256 devices in a mesh: leaf: 128 (over y, x, z), col: 2 (over core).
Axes of the slice: x: 4, y: 4, z: 8, core: 2. Of those that a mesh axis runs over, the one named last changes fastest.
Arguments:
- sources: bfloat16 [524288, 256], P('leaf', 'col'), may hold values from -6 to 6
- near_tiles: bfloat16 [2048, 8, 256, 256], P('leaf', 'col'), may hold values from -0.125 to 0.125
- near_index: int32 [2048, 8], P('leaf'), may hold values from 0 to 2047, as said below
- near_count: int32 [2048], P('leaf'), may hold values from 1 to 8, as said below
- leaf_basis: bfloat16 [2048, 64, 256], P('leaf'), may hold values from -0.375 to 0.375
- leaf_coupling: bfloat16 [2048, 64, 256], P('leaf'), may hold values from -0.375 to 0.375
- leaf_far: int32 [2048, 4], P('leaf'), may hold values from 0 to 2047, as said below
- up_leaf: bfloat16 [256, 64, 512], P('leaf'), may hold values from -0.25 to 0.25
- mid_coupling: bfloat16 [256, 64, 256], P('leaf'), may hold values from -0.375 to 0.375
- mid_far: int32 [256, 4], P('leaf'), may hold values from 0 to 255, as said below
- up_mid: bfloat16 [256, 64, 64], P('leaf'), may hold values from -0.75 to 0.75
- top_coupling: bfloat16 [32, 64, 2048], replicated, may hold values from -0.125 to 0.125
Outputs:
- product: float32 [524288, 256], P('leaf', 'col')
The draws below stay inside these ranges and needn't reach their ends.
Inputs may be any that keep to these rules, and one draw needn't show every extreme that they name: `near_index`: entry 0 of row i is i; the other 7 entries are distinct leaves j with j != i and |i - j| <= 8. Only the first near_count[i] slots of leaf i count; some leaf has all 8. `leaf_far`: row i holds 4 distinct leaves j != i with |i // 8 - j // 8| <= 1. `mid_far`: row a holds 4 distinct middle clusters b != a with |a // 8 - b // 8| <= 1.
All inputs are finite; a program needn't handle non-finite values.
Results may differ from the reference program's by a relative error of at most 0.01.
Values may be sent and summed in bfloat16 or wider, within the bound.
A program may use at most 128 MiB of HBM per device.

```python
import jax
import jax.numpy as jnp
from jax import lax

LEAF = 256
RANK = 64
COLS = 256
CHILD = 8
NEAR = 8
FAR = 4
LEAVES_DEV = 16
NL = 2048
NL1 = 256
NL2 = 32
N = 524288


def window_pick(seed_key, row_count, slot_count, near_only):
    span = 2 * CHILD - 1
    offsets = jnp.arange(-span, span + 1, dtype=jnp.int32)
    rows_ids = jnp.arange(row_count, dtype=jnp.int32)[:, None]
    target = rows_ids + offsets[None, :]
    inside = (target >= 0) & (target < row_count) & (offsets[None, :] != 0)
    if near_only:
        inside = inside & (jnp.abs(offsets)[None, :] <= CHILD)
    else:
        inside = inside & (jnp.abs(rows_ids // CHILD - target // CHILD) <= 1)
    scores = jax.random.randint(seed_key, target.shape, 0, 1 << 20, dtype=jnp.int32) * 64 + jnp.arange(offsets.shape[0], dtype=jnp.int32)[None, :]
    scores = jnp.where(inside, scores, -1)
    _, chosen = lax.top_k(scores, slot_count)
    return jnp.take_along_axis(target, chosen, axis=1).astype(jnp.int32)


def draw_near_index(key, part):
    picked = window_pick(jax.random.fold_in(key, 11), NL, NEAR - 1, True)
    itself = jnp.arange(NL, dtype=jnp.int32)[:, None]
    return jnp.concatenate([itself, picked], axis=1).astype(jnp.int32)


def draw_near_count(key, part):
    device_level = jax.random.randint(jax.random.fold_in(key, 12), (NL // LEAVES_DEV,), 1, NEAR + 1, dtype=jnp.int32)
    jitter = jax.random.randint(jax.random.fold_in(key, 13), (NL,), -1, 2, dtype=jnp.int32)
    counts = jnp.clip(jnp.repeat(device_level, LEAVES_DEV) + jitter, 1, NEAR)
    fullest = jax.random.randint(jax.random.fold_in(key, 14), (), 0, NL, dtype=jnp.int32)
    return counts.at[fullest].set(NEAR).astype(jnp.int32)


def draw_leaf_far(key, part):
    return window_pick(jax.random.fold_in(key, 15), NL, FAR, False)


def draw_mid_far(key, part):
    return window_pick(jax.random.fold_in(key, 16), NL1, FAR, False)


def block_levels(own_key, shape, pieces, smallest, high):
    level = 1.0
    for axis_at, blocks in pieces:
        draws = jax.random.uniform(jax.random.fold_in(jax.random.fold_in(own_key, 6), axis_at), (blocks,), jnp.float32, smallest / len(pieces), high / len(pieces))
        level = level * jnp.repeat(jnp.exp(draws), shape[axis_at] // blocks).reshape((-1,) + (1,) * (len(shape) - 1 - axis_at))
    return level


def bell_draw(stream_key, shape, deviation, most, cuts=(), held_as=jnp.bfloat16):
    entries = deviation * jax.random.normal(stream_key, shape, jnp.float32)
    if cuts:
        entries = entries * block_levels(stream_key, shape, cuts, -0.22, 0.18)
    return jnp.clip(entries, -most, most).astype(held_as)


def setup_inputs(seed: int = 0) -> dict:
    key_of = jax.random.split(jax.random.key(seed), 13)
    sources = bell_draw(key_of[0], (N, COLS), 1.0, 6.0, ((0, 128), (1, 2)))
    near_tiles = bell_draw(key_of[1], (NL, NEAR, LEAF, LEAF), (LEAF * NEAR) ** -0.5, 0.125, ((0, 128), (1, 2)))
    near_index = draw_near_index(jax.random.fold_in(key_of[12], 71), 0)
    near_count = draw_near_count(jax.random.fold_in(key_of[12], 71), 0)
    leaf_basis = bell_draw(key_of[4], (NL, RANK, LEAF), LEAF ** -0.5, 0.375, ((0, 128),))
    leaf_coupling = bell_draw(key_of[5], (NL, RANK, FAR * RANK), (FAR * RANK) ** -0.5, 0.375, ((0, 128),))
    leaf_far = draw_leaf_far(jax.random.fold_in(key_of[12], 71), 0)
    up_leaf = bell_draw(key_of[7], (NL1, RANK, CHILD * RANK), (CHILD * RANK) ** -0.5, 0.25, ((0, 128),))
    mid_coupling = bell_draw(key_of[8], (NL1, RANK, FAR * RANK), (FAR * RANK) ** -0.5, 0.375, ((0, 128),))
    mid_far = draw_mid_far(jax.random.fold_in(key_of[12], 71), 0)
    up_mid = bell_draw(key_of[10], (NL1, RANK, RANK), RANK ** -0.5, 0.75, ((0, 128),))
    top_coupling = bell_draw(key_of[11], (NL2, RANK, NL2 * RANK), ((NL2 - 1) * RANK) ** -0.5, 0.125)
    return dict(sources=sources, near_tiles=near_tiles, near_index=near_index, near_count=near_count, leaf_basis=leaf_basis, leaf_coupling=leaf_coupling, leaf_far=leaf_far, up_leaf=up_leaf, mid_coupling=mid_coupling, mid_far=mid_far, up_mid=up_mid, top_coupling=top_coupling)


def reference(sources, near_tiles, near_index, near_count, leaf_basis, leaf_coupling, leaf_far, up_leaf, mid_coupling, mid_far, up_mid, top_coupling):
    f32 = jnp.float32
    bf16 = jnp.bfloat16
    blocks = sources.astype(f32).reshape(NL, LEAF, COLS)
    leaf_coef = jnp.einsum("lrk,lkc->lrc", leaf_basis.astype(f32), blocks).astype(bf16)
    mid_coef = jnp.einsum("qrk,qkc->qrc", up_leaf.astype(f32), leaf_coef.astype(f32).reshape(NL1, CHILD * RANK, COLS)).astype(bf16)
    mid_lift = jnp.einsum("qrs,qsc->qrc", up_mid.astype(f32), mid_coef.astype(f32)).astype(bf16)
    top_sum = jnp.sum(mid_lift.astype(f32).reshape(NL2, CHILD, RANK, COLS), axis=1)
    top_coef = top_sum.astype(bf16)
    top_ids = jnp.arange(NL2)
    keep_mask = top_ids[:, None] != top_ids[None, :]
    stacked = jnp.where(keep_mask[:, :, None, None], top_coef.astype(f32)[None], jnp.zeros((), f32))
    top_field = jnp.einsum("prk,pkc->prc", top_coupling.astype(f32), stacked.reshape(NL2, NL2 * RANK, COLS)).astype(bf16)
    mid_picked = mid_coef.astype(f32)[mid_far].reshape(NL1, FAR * RANK, COLS)
    mid_parent = jnp.arange(NL1) // CHILD
    mid_field = (jnp.einsum("qrk,qkc->qrc", mid_coupling.astype(f32), mid_picked)
                 + jnp.einsum("qrs,qrc->qsc", up_mid.astype(f32), top_field.astype(f32)[mid_parent])).astype(bf16)
    leaf_picked = leaf_coef.astype(f32)[leaf_far].reshape(NL, FAR * RANK, COLS)
    down_part = jnp.einsum("qrs,qrc->qsc", up_leaf.astype(f32), mid_field.astype(f32)).reshape(NL, RANK, COLS)
    leaf_field = (jnp.einsum("lrk,lkc->lrc", leaf_coupling.astype(f32), leaf_picked) + down_part).astype(bf16)
    far_part = jnp.einsum("lrk,lrc->lkc", leaf_basis.astype(f32), leaf_field.astype(f32)).reshape(N, COLS)

    def per_leaf(inputs):
        tile_set, index_row, live_count = inputs
        picked = blocks[index_row]
        live_mask = jnp.arange(NEAR) < live_count
        picked = jnp.where(live_mask[:, None, None], picked, jnp.zeros((), f32))
        return jnp.einsum("sij,sjc->ic", tile_set.astype(f32), picked)

    near_part = lax.map(per_leaf, (near_tiles, near_index, near_count)).reshape(N, COLS)
    return near_part + far_part
```

```python
import functools

import jax
import jax.numpy as jnp
from jax import lax
from jax.experimental import pallas as pl
from jax.experimental.pallas import tpu as pltpu
from jax.sharding import PartitionSpec as P

MESH = pl.DeviceIdType.MESH
F32 = jnp.float32
BF16 = jnp.bfloat16

LEAF = 256
RANK = 64
HALF = 128
OWN = 16
HALO = 8
MIDS = 2
GROUP = 4
TOPS = 32
SLOTS = 4
ZERO = OWN + 2 * HALO
CHUNK = 2
CHUNKS = HALO // CHUNK


def dot(a, b):
    return jnp.dot(a, b, preferred_element_type=F32)


def dot_t(a, b):
    return lax.dot_general(a, b, (((0,), (0,)), ((), ())), preferred_element_type=F32)


def kernel(
    src, tiles, near_index, near_count, basis, coupling, leaf_far, up_leaf, mid_coupling, mid_far, up_mid, top_coupling,
    out,
    w0, w1, tile, bas, cpl, upl, mcp, upm, top, coef, mid, part, top_a, coef_top, top_b, field, top_c, mfield,
    lfield, near, give, take,
    load_sem, tile_sem, out_sem, sib_send, sib_recv, halo_send, halo_recv, fwd_send, fwd_recv,
    coef_send, coef_recv, mid_send, mid_recv, a_send, a_recv, b_send, b_recv, c_send, c_recv, give_send, give_recv,
):
    d, c = lax.axis_index("leaf"), lax.axis_index("col")
    devices = TOPS * GROUP
    g, r = d // GROUP, d % GROUP
    z, x, y = g % 2, (g // 2) % 4, g // 8
    sibling = (d, 1 - c)
    after, before = ((d + 1) % devices, c), ((d + devices - 1) % devices, c)

    def member(group, k):
        return (group * GROUP + k, c)

    mates = [member(g, (r + o) % GROUP) for o in (1, 2, 3)]
    sides = [member((g + o) % TOPS, k) for o in (1, TOPS - 1) for k in range(GROUP)]
    far_x, far_r = (x + r) % 4, (GROUP - r) % GROUP
    peers = [(j, zt, member((((y + j) % 4) * 4 + far_x) * 2 + zt, far_r)) for j in range(4) for zt in range(2)]

    def copy(a, b, send, recv, device):
        return pltpu.make_async_remote_copy(
            src_ref=a, dst_ref=b, send_sem=send, recv_sem=recv, device_id=device, device_id_type=MESH
        )

    def not_self(j, zt, body):
        if j == 0:
            pl.when(jnp.logical_or(r != 0, z != zt))(body)
        else:
            body()

    barrier = pltpu.get_barrier_semaphore()

    def greet(device):
        pl.semaphore_signal(barrier, inc=1, device_id=device, device_id_type=MESH)

    for device in [sibling] + mates + sides:
        greet(device)
    for j, zt, device in peers:
        not_self(j, zt, functools.partial(greet, device))

    loads = [
        pltpu.make_async_copy(src, w0.at[pl.ds(HALO, OWN)], load_sem.at[0]),
        pltpu.make_async_copy(basis, bas, load_sem.at[1]),
        pltpu.make_async_copy(up_leaf, upl, load_sem.at[2]),
        pltpu.make_async_copy(up_mid, upm, load_sem.at[3]),
        pltpu.make_async_copy(coupling, cpl, load_sem.at[4]),
        pltpu.make_async_copy(mid_coupling, mcp, load_sem.at[5]),
    ]
    for j in range(4):
        pair = ((y + j) % 4) * 4 + far_x
        loads.append(
            pltpu.make_async_copy(
                top_coupling.at[g, :, pl.ds(pl.multiple_of(pair * 2 * RANK, 2 * RANK), 2 * RANK)],
                top.at[j],
                load_sem.at[6 + j],
            )
        )
    for load in loads:
        load.start()
    tile_loads = [
        pltpu.make_async_copy(tiles.at[pl.ds(4 * k, 4)], tile.at[pl.ds(4 * k, 4)], tile_sem.at[k]) for k in range(4)
    ]
    for load in tile_loads:
        load.start()

    zero = jnp.zeros((LEAF, HALF), BF16)
    w0[ZERO] = zero
    w1[ZERO] = zero

    @pl.when(r == 0)
    def _():
        top_b[0, z] = jnp.zeros((RANK, HALF), BF16)
        pl.semaphore_wait(barrier, 19)

    @pl.when(r != 0)
    def _():
        pl.semaphore_wait(barrier, 20)

    to_sibling = copy(src, w1.at[pl.ds(HALO, OWN)], sib_send, sib_recv, sibling)
    to_after, to_before, fwd_low, fwd_high = [], [], [], []
    for i in range(CHUNKS):
        low = pl.ds(HALO - CHUNK * (i + 1), CHUNK)
        high = pl.ds(HALO + OWN + CHUNK * i, CHUNK)
        to_after.append(
            copy(src.at[pl.ds(OWN - CHUNK * (i + 1), CHUNK)], w0.at[low], halo_send.at[0, i], halo_recv.at[0, i], after)
        )
        to_before.append(
            copy(src.at[pl.ds(CHUNK * i, CHUNK)], w0.at[high], halo_send.at[1, i], halo_recv.at[1, i], before)
        )
        fwd_low.append(copy(w0.at[low], w1.at[low], fwd_send.at[0, i], fwd_recv.at[0, i], sibling))
        fwd_high.append(copy(w0.at[high], w1.at[high], fwd_send.at[1, i], fwd_recv.at[1, i], sibling))
    for i in range(CHUNKS):
        to_after[i].start()
        to_before[i].start()
    to_sibling.start()

    loads[0].wait()
    loads[1].wait()

    def leaf_step(i, _):
        coef[HALO + i] = dot(bas[i], w0[HALO + i]).astype(BF16)
        return 0

    lax.fori_loop(0, OWN, leaf_step, 0)
    coef_out = [
        copy(coef.at[pl.ds(OWN, HALO)], coef.at[pl.ds(0, HALO)], coef_send.at[0], coef_recv.at[0], after),
        copy(coef.at[pl.ds(HALO, HALO)], coef.at[pl.ds(HALO + OWN, HALO)], coef_send.at[1], coef_recv.at[1], before),
    ]

    loads[2].wait()
    loads[3].wait()
    own_mid = pl.ds(MIDS * (GROUP + r), MIDS)
    total = None
    for q in range(MIDS):
        rows = coef[pl.ds(HALO + 8 * q, 8)].reshape(8 * RANK, HALF)
        value = dot(upl[q], rows).astype(BF16)
        mid[MIDS * (GROUP + r) + q] = value
        lift = dot(upm[q], value).astype(BF16).astype(F32)
        total = lift if total is None else total + lift
    part[...] = total
    to_mates = [copy(part, top_a.at[o], a_send.at[o], a_recv.at[o], mates[o]) for o in range(3)]
    for one in to_mates:
        one.start()
    mid_out = []
    for o in range(3):
        mid_out.append(copy(mid.at[own_mid], mid.at[own_mid], mid_send.at[o], mid_recv.at[GROUP + r], mates[o]))
    for o, base in ((0, 0), (1, 2 * GROUP)):
        there = pl.ds(MIDS * (base + r), MIDS)
        for k in range(GROUP):
            n = 3 + GROUP * o + k
            mid_out.append(
                copy(mid.at[own_mid], mid.at[there], mid_send.at[n], mid_recv.at[base + r], sides[GROUP * o + k])
            )
    for one in coef_out:
        one.start()
    for one in mid_out:
        one.start()

    for one in to_mates:
        one.wait_recv()
    coef_top[...] = (part[...] + top_a[0] + top_a[1] + top_a[2]).astype(BF16)
    to_peers = []
    for j, zt, device in peers:
        one = copy(
            coef_top, top_b.at[(4 - j) % 4, z], b_send.at[j, zt], b_recv.at[(4 - j) % 4, z], device
        )
        to_peers.append((j, zt, one))
        not_self(j, zt, one.start)

    for i in range(2):
        to_after[i].wait_recv()
        to_before[i].wait_recv()
        fwd_low[i].start()
        fwd_high[i].start()
    loads[4].wait()
    for one in coef_out:
        one.wait_recv()

    def far_step(i, _):
        picked = [coef[jnp.clip(leaf_far[i, f] - (d * OWN - HALO), 0, ZERO - 1)] for f in range(4)]
        lfield[i] = dot(cpl[i], jnp.concatenate(picked, axis=0))
        return 0

    lax.fori_loop(0, OWN, far_step, 0)

    for j in range(4):
        loads[6 + j].wait()
    for j, zt, _ in peers:
        got = copy(coef_top, top_b.at[j, zt], b_send.at[j, zt], b_recv.at[j, zt], sibling)
        not_self(j, zt, got.wait_recv)
    total = dot(top[0], top_b[0].reshape(2 * RANK, HALF))
    for j in range(1, 4):
        total = total + dot(top[j], top_b[j].reshape(2 * RANK, HALF))
    field[...] = total
    fields_out = [copy(field, top_c.at[o], c_send.at[o], c_recv.at[o], mates[o]) for o in range(3)]
    for one in fields_out:
        one.start()

    for k in range(3 * GROUP):
        here = mid.at[pl.ds(MIDS * k, MIDS)]
        got = copy(here, here, mid_send.at[0], mid_recv.at[k], sibling)
        if k // GROUP == 1:
            pl.when(k != GROUP + r)(got.wait_recv)
        else:
            got.wait_recv()
    loads[5].wait()
    first = (g - 1) * 8
    for q in range(MIDS):
        picked = [mid[jnp.clip(mid_far[q, f] - first, 0, 3 * GROUP * MIDS - 1)] for f in range(4)]
        mfield[q] = dot(mcp[q], jnp.concatenate(picked, axis=0))
    for one in fields_out:
        one.wait_recv()
    top_field = (field[...] + top_c[0] + top_c[1] + top_c[2]).astype(BF16)
    for q in range(MIDS):
        value = (mfield[q] + dot_t(upm[q], top_field)).astype(BF16)
        down = dot_t(upl[q], value).reshape(8, RANK, HALF)
        lfield[pl.ds(8 * q, 8)] = lfield[pl.ds(8 * q, 8)] + down

    for i in range(2, CHUNKS):
        to_after[i].wait_recv()
        to_before[i].wait_recv()
        fwd_low[i].start()
        fwd_high[i].start()

    def product_step(i, _):
        near[i] = dot_t(bas[i], lfield[i].astype(BF16))
        return 0

    lax.fori_loop(0, OWN, product_step, 0)

    to_sibling.wait_recv()
    for i in range(CHUNKS):
        fwd_low[i].wait_recv()
        fwd_high[i].wait_recv()
    for load in tile_loads:
        load.wait()

    def give_copy(i):
        return copy(give.at[i], take.at[i], give_send.at[i], give_recv.at[i], sibling)

    def near_step(i, _):
        total = None
        for s in range(SLOTS):
            slot = c * SLOTS + s
            j = jnp.clip(near_index[i, slot] - (d * OWN - HALO), 0, ZERO - 1)
            j = jnp.where(slot < near_count[i], j, ZERO)
            rows = jnp.concatenate([w0[j], w1[j]], axis=1)
            term = dot(tile[i, s], rows)
            total = term if total is None else total + term
        near[i] = near[i] + total[:, :HALF]
        give[i] = total[:, HALF:].astype(BF16)
        give_copy(i).start()
        return 0

    lax.fori_loop(0, OWN, near_step, 0)

    def finish(i, _):
        give_copy(i).wait_recv()
        near[i] = near[i] + take[i].astype(F32)
        pltpu.make_async_copy(near.at[i], out.at[i], out_sem.at[i]).start()
        return 0

    lax.fori_loop(0, OWN, finish, 0)

    def drain(i, _):
        pltpu.make_async_copy(near.at[i], out.at[i], out_sem.at[i]).wait()
        give_copy(i).wait_send()
        return 0

    lax.fori_loop(0, OWN, drain, 0)
    to_sibling.wait_send()
    for one in to_after + to_before + fwd_low + fwd_high + coef_out + mid_out + to_mates + fields_out:
        one.wait_send()
    for j, zt, one in to_peers:
        not_self(j, zt, one.wait_send)


def shards(
    sources, near_tiles, near_index, near_count, leaf_basis, leaf_coupling, leaf_far, up_leaf, mid_coupling, mid_far,
    up_mid, top_coupling,
):
    any_spec = pl.BlockSpec(memory_space=pl.ANY)
    smem_spec = pl.BlockSpec(memory_space=pltpu.SMEM)
    dma, vmem = pltpu.SemaphoreType.DMA, pltpu.VMEM
    window = OWN + 2 * HALO
    result = pl.pallas_call(
        kernel,
        out_shape=jax.ShapeDtypeStruct((OWN, LEAF, HALF), F32),
        in_specs=[
            any_spec, any_spec, smem_spec, smem_spec, any_spec, any_spec, smem_spec, any_spec, any_spec, smem_spec,
            any_spec, any_spec,
        ],
        out_specs=any_spec,
        scratch_shapes=[
            vmem((window + 1, LEAF, HALF), BF16),
            vmem((window + 1, LEAF, HALF), BF16),
            vmem((OWN, SLOTS, LEAF, LEAF), BF16),
            vmem((OWN, RANK, LEAF), BF16),
            vmem((OWN, RANK, 4 * RANK), BF16),
            vmem((MIDS, RANK, 8 * RANK), BF16),
            vmem((MIDS, RANK, 4 * RANK), BF16),
            vmem((MIDS, RANK, RANK), BF16),
            vmem((4, RANK, 2 * RANK), BF16),
            vmem((window, RANK, HALF), BF16),
            vmem((3 * GROUP * MIDS, RANK, HALF), BF16),
            vmem((RANK, HALF), F32),
            vmem((3, RANK, HALF), F32),
            vmem((RANK, HALF), BF16),
            vmem((4, 2, RANK, HALF), BF16),
            vmem((RANK, HALF), F32),
            vmem((3, RANK, HALF), F32),
            vmem((MIDS, RANK, HALF), F32),
            vmem((OWN, RANK, HALF), F32),
            vmem((OWN, LEAF, HALF), F32),
            vmem((OWN, LEAF, HALF), BF16),
            vmem((OWN, LEAF, HALF), BF16),
            dma((10,)), dma((4,)), dma((OWN,)),
            dma(()), dma(()),
            dma((2, CHUNKS)), dma((2, CHUNKS)),
            dma((2, CHUNKS)), dma((2, CHUNKS)),
            dma((2,)), dma((2,)),
            dma((11,)), dma((3 * GROUP,)),
            dma((3,)), dma((3,)),
            dma((4, 2)), dma((4, 2)),
            dma((3,)), dma((3,)),
            dma((OWN,)), dma((OWN,)),
        ],
        compiler_params=pltpu.CompilerParams(
            collective_id=0, has_side_effects=True, vmem_limit_bytes=48 * 2**20
        ),
        name="h2_product",
    )(
        sources.reshape(OWN, LEAF, HALF), near_tiles, near_index, near_count, leaf_basis, leaf_coupling, leaf_far,
        up_leaf, mid_coupling, mid_far, up_mid, top_coupling,
    )
    return result.reshape(OWN * LEAF, HALF)


def solution(mesh):
    return jax.shard_map(
        shards,
        mesh=mesh,
        in_specs=(
            P("leaf", "col"),
            P("leaf", "col", None, None),
            P("leaf", None),
            P("leaf"),
            P("leaf", None, None),
            P("leaf", None, None),
            P("leaf", None),
            P("leaf", None, None),
            P("leaf", None, None),
            P("leaf", None),
            P("leaf", None, None),
            P(),
        ),
        out_specs=P("leaf", "col"),
        check_vma=False,
    )
```

```python
import functools

import jax
import jax.numpy as jnp
from jax import lax
from jax.experimental import pallas as pl
from jax.experimental.pallas import tpu as pltpu
from jax.sharding import PartitionSpec as P

MESH = pl.DeviceIdType.MESH
F32 = jnp.float32
BF16 = jnp.bfloat16

LEAF = 256
RANK = 64
HALF = 128
OWN = 16
HALO = 8
MIDS = 2
GROUP = 4
RING = 8
COLUMNS = 16
SLOTS = 4
WINDOW = OWN + 2 * HALO
CHUNK = 2
CHUNKS = HALO // CHUNK
MID_WINDOW = 4 * GROUP * MIDS


def dot(a, b):
    return jnp.dot(a, b, preferred_element_type=F32)


def dot_t(a, b):
    return lax.dot_general(a, b, (((0,), (0,)), ((), ())), preferred_element_type=F32)


def by_fours(body):
    def step(k, _):
        for i in range(4):
            body(4 * k + i)
        return 0

    lax.fori_loop(0, OWN // 4, step, 0)


def kernel(
    src, tiles, near_index_in, near_count_in, basis, coupling, leaf_far_in, up_leaf, mid_coupling, mid_far_in, up_mid,
    top_coupling,
    near, take,
    near_index, near_count, leaf_far, mid_far,
    w0, w1, tile, bas, cpl, upl, mcp, upm, top, coef, mid, part, top_a, coef_top, top_b, field, top_c, lfield, give,
    load_sem, tile_sem, sib_send, sib_recv, halo_send, halo_recv, fwd_send, fwd_recv, coef_send, coef_recv,
    ring_send, ring_recv, a_send, a_recv, b_send, b_recv, c_send, c_recv, give_send, give_recv,
):
    d, c = lax.axis_index("leaf"), lax.axis_index("col")
    devices = COLUMNS * RING
    g, r = d // GROUP, d % GROUP
    column, z = d // RING, d % RING
    half, x, y = g % 2, column % 4, column // 4
    sibling = (d, 1 - c)
    after, before = ((d + 1) % devices, c), ((d + devices - 1) % devices, c)
    above, below = (column * RING + (z + 1) % RING, c), (column * RING + (z + RING - 1) % RING, c)
    mates = [(g * GROUP + (r + o) % GROUP, c) for o in (1, 2, 3)]
    inner = (r * (3 - r)) // 2
    other = column * RING + (1 - half) * GROUP
    sums = [(g * GROUP + 1, c), (g * GROUP + 2, c), (other, c), (other + 3, c)]
    sum_of = inner * half + (1 - inner) * (1 - half)
    odd = r // 2
    peers = [
        (((((y + 2 * jj + odd) % 4) * 4 + (x + xo) % 4) * RING + z), jj, xo) for jj in range(2) for xo in range(4)
    ]
    across = (((column + 1 - 2 * half + COLUMNS) % COLUMNS) * RING + z, c)
    across_from = (((column - 1 + 2 * half + COLUMNS) % COLUMNS) * RING + z, c)

    def copy(a, b, send, recv, device):
        return pltpu.make_async_remote_copy(
            src_ref=a, dst_ref=b, send_sem=send, recv_sem=recv, device_id=device, device_id_type=MESH
        )

    def if_not(flag, here, body):
        if here:
            pl.when(jnp.logical_not(flag))(body)
        else:
            body()

    barrier = pltpu.get_barrier_semaphore()

    def greet(device):
        pl.semaphore_signal(barrier, inc=1, device_id=device, device_id_type=MESH)

    column_mates = [(column * RING + (z + o) % RING, c) for o in range(1, RING)]
    for device in [sibling, after, before, across, across_from] + column_mates:
        greet(device)
    for device, jj, xo in peers:
        if_not(odd == 0, jj == 0 and xo == 0, functools.partial(greet, (device, c)))

    loads = [
        pltpu.make_async_copy(src, w0.at[pl.ds(HALO, OWN)], load_sem.at[0]),
        pltpu.make_async_copy(basis, bas, load_sem.at[1]),
        pltpu.make_async_copy(up_leaf, upl, load_sem.at[2]),
        pltpu.make_async_copy(up_mid, upm, load_sem.at[3]),
        pltpu.make_async_copy(leaf_far_in, leaf_far, load_sem.at[4]),
        pltpu.make_async_copy(mid_far_in, mid_far, load_sem.at[5]),
        pltpu.make_async_copy(near_index_in, near_index, load_sem.at[6]),
        pltpu.make_async_copy(near_count_in, near_count, load_sem.at[7]),
        pltpu.make_async_copy(coupling, cpl, load_sem.at[8]),
        pltpu.make_async_copy(mid_coupling, mcp, load_sem.at[9]),
    ]
    for device, jj, xo in peers:
        pair = ((y + 2 * jj + odd) % 4) * 4 + (x + xo) % 4
        loads.append(
            pltpu.make_async_copy(
                top_coupling.at[g, :, pl.ds(pl.multiple_of(pair * 2 * RANK, 2 * RANK), 2 * RANK)],
                top.at[4 * jj + xo],
                load_sem.at[10 + 4 * jj + xo],
            )
        )
    for load in loads:
        load.start()
    tile_loads = [
        pltpu.make_async_copy(tiles.at[pl.ds(4 * k, 4)], tile.at[pl.ds(4 * k, 4)], tile_sem.at[k]) for k in range(4)
    ]
    for load in tile_loads:
        load.start()

    zero = jnp.zeros((LEAF, HALF), BF16)
    w0[WINDOW] = zero
    w1[WINDOW] = zero
    for n in range(8):
        top_b[n, 1 - sum_of] = jnp.zeros((RANK, HALF), BF16)

    @pl.when(odd == 0)
    def _():
        top_b[0, sum_of] = jnp.zeros((RANK, HALF), BF16)
        pl.semaphore_wait(barrier, 19)

    @pl.when(odd != 0)
    def _():
        pl.semaphore_wait(barrier, 20)

    to_sibling = copy(src, w1.at[pl.ds(HALO, OWN)], sib_send, sib_recv, sibling)
    to_after, to_before, fwd_low, fwd_high = [], [], [], []
    for i in range(CHUNKS):
        low = pl.ds(HALO - CHUNK * (i + 1), CHUNK)
        high = pl.ds(HALO + OWN + CHUNK * i, CHUNK)
        to_after.append(
            copy(src.at[pl.ds(OWN - CHUNK * (i + 1), CHUNK)], w0.at[low], halo_send.at[0, i], halo_recv.at[0, i], after)
        )
        to_before.append(
            copy(src.at[pl.ds(CHUNK * i, CHUNK)], w0.at[high], halo_send.at[1, i], halo_recv.at[1, i], before)
        )
        fwd_low.append(copy(w0.at[low], w1.at[low], fwd_send.at[0, i], fwd_recv.at[0, i], sibling))
        fwd_high.append(copy(w0.at[high], w1.at[high], fwd_send.at[1, i], fwd_recv.at[1, i], sibling))

    def forward(i):
        to_after[i].wait_recv()
        to_before[i].wait_recv()
        fwd_low[i].start()
        fwd_high[i].start()

    for i in range(CHUNKS):
        to_after[i].start()
        to_before[i].start()
    to_sibling.start()

    loads[0].wait()
    loads[1].wait()

    def leaf_step(i):
        coef[HALO + i] = dot(bas[i], w0[HALO + i]).astype(BF16)

    by_fours(leaf_step)
    coef_out = [
        copy(coef.at[pl.ds(OWN, HALO)], coef.at[pl.ds(0, HALO)], coef_send.at[0], coef_recv.at[0], after),
        copy(coef.at[pl.ds(HALO, HALO)], coef.at[pl.ds(HALO + OWN, HALO)], coef_send.at[1], coef_recv.at[1], before),
    ]

    loads[2].wait()
    loads[3].wait()
    base = GROUP * MIDS
    values = [
        dot(upl[q], coef[pl.ds(HALO + 8 * q, 8)].reshape(8 * RANK, HALF)).astype(BF16) for q in range(MIDS)
    ]
    lifts = [dot(upm[q], values[q]).astype(BF16).astype(F32) for q in range(MIDS)]
    part[...] = (lifts[0] + lifts[1]).astype(BF16)
    for q in range(MIDS):
        mid[base + MIDS * z + q] = values[q]
    sums_out = [copy(part, top_a.at[r], a_send.at[n], a_recv.at[r], sums[n]) for n in range(4)]
    for n in range(4):
        if_not(r == n + 1, n < 2, sums_out[n].start)

    def of(origin):
        return mid.at[pl.ds(base + MIDS * ((origin + RING) % RING), MIDS)]

    ring_up = [copy(of(z - s), of(z - s), ring_send.at[0, s], ring_recv.at[0, s], above) for s in range(4)]
    ring_down = [copy(of(z + s), of(z + s), ring_send.at[1, s], ring_recv.at[1, s], below) for s in range(3)]
    got_up = [copy(of(z - s - 1), of(z - s - 1), ring_send.at[0, s], ring_recv.at[0, s], above) for s in range(4)]
    got_down = [copy(of(z + s + 1), of(z + s + 1), ring_send.at[1, s], ring_recv.at[1, s], below) for s in range(3)]
    ring_up[0].start()
    ring_down[0].start()
    for one in coef_out:
        one.start()

    for n in range(GROUP):
        got = copy(part, top_a.at[n], a_send.at[0], a_recv.at[n], sibling)
        pl.when(jnp.logical_or(inner == 0, r != n))(got.wait_recv)

    @pl.when(inner == 1)
    def _():
        top_a[r] = part[...]

    total = (top_a[0].astype(F32) + top_a[1].astype(F32)) + (top_a[2].astype(F32) + top_a[3].astype(F32))
    coef_top[...] = total.astype(BF16)
    to_peers = []
    for device, jj, xo in peers:
        slot = 4 * ((jj + odd) % 2) + (4 - xo) % 4
        one = copy(coef_top, top_b.at[slot, sum_of], b_send.at[4 * jj + xo], b_recv.at[slot], (device, c))
        to_peers.append(one)
        if_not(odd == 0, jj == 0 and xo == 0, one.start)

    @pl.when(r == 0)
    def _():
        top_b[0, sum_of] = coef_top[...]

    got_up[0].wait_recv()
    ring_up[1].start()
    got_down[0].wait_recv()
    ring_down[1].start()
    forward(0)

    loads[4].wait()
    loads[8].wait()
    for one in coef_out:
        one.wait_recv()

    def far_step(i):
        picked = [coef[jnp.clip(leaf_far[f, i] - (d * OWN - HALO), 0, WINDOW - 1)] for f in range(4)]
        lfield[i] = dot(cpl[i], jnp.concatenate(picked, axis=0))

    by_fours(far_step)
    got_up[1].wait_recv()
    ring_up[2].start()
    got_down[1].wait_recv()
    ring_down[2].start()

    for n in range(8):
        loads[10 + n].wait()
    for n in range(8):
        got = copy(coef_top, top_b.at[n, sum_of], b_send.at[n], b_recv.at[n], sibling)
        if_not(odd == 0, n == 0, got.wait_recv)
    terms = [dot(top[n], top_b[n].reshape(2 * RANK, HALF)) for n in range(8)]
    total = ((terms[0] + terms[1]) + (terms[2] + terms[3])) + ((terms[4] + terms[5]) + (terms[6] + terms[7]))
    field[...] = total.astype(BF16)
    fields_out = [copy(field, top_c.at[o], c_send.at[o], c_recv.at[o], mates[o]) for o in range(3)]
    for one in fields_out:
        one.start()
    got_up[2].wait_recv()
    ring_up[3].start()
    got_down[2].wait_recv()
    forward(1)
    got_up[3].wait_recv()

    theirs = mid.at[pl.ds(base + (1 - half) * base, base)]
    there = mid.at[pl.ds(3 * base * half, base)]
    cross = copy(
        theirs, mid.at[pl.ds(3 * base * half, base)], ring_send.at[1, 3], ring_recv.at[1, 3], across
    )
    cross.start()
    for one in fields_out:
        one.wait_recv()
    top_field = ((total + top_c[0].astype(F32)) + (top_c[1].astype(F32) + top_c[2].astype(F32))).astype(BF16)
    lifted = [dot_t(upm[q], top_field) for q in range(MIDS)]
    forward(2)

    loads[5].wait()
    loads[9].wait()
    copy(theirs, there, ring_send.at[1, 3], ring_recv.at[1, 3], across).wait_recv()
    first = column * RING * MIDS - base
    for q in range(MIDS):
        picked = [mid[jnp.clip(mid_far[q, f] - first, 0, MID_WINDOW - 1)] for f in range(4)]
        value = (dot(mcp[q], jnp.concatenate(picked, axis=0)) + lifted[q]).astype(BF16)
        down = dot_t(upl[q], value).reshape(8, RANK, HALF)
        lfield[pl.ds(8 * q, 8)] = lfield[pl.ds(8 * q, 8)] + down
    forward(3)

    loads[6].wait()
    loads[7].wait()
    to_sibling.wait_recv()
    for i in range(CHUNKS):
        fwd_low[i].wait_recv()
        fwd_high[i].wait_recv()
    for load in tile_loads:
        load.wait()

    def give_copy(i):
        return copy(give.at[i], take.at[i], give_send.at[i], give_recv.at[i], sibling)

    def near_leaf(i):
        terms = []
        for s in range(SLOTS):
            slot = c * SLOTS + s
            j = jnp.clip(near_index[slot, i] - (d * OWN - HALO), 0, WINDOW - 1)
            j = jnp.where(slot < near_count[i], j, WINDOW)
            terms.append(dot(tile[i, s], jnp.concatenate([w0[j], w1[j]], axis=1)))
        total = (terms[0] + terms[1]) + (terms[2] + terms[3])
        give[i] = total[:, HALF:].astype(BF16)
        give_copy(i).start()
        near[i] = total[:, :HALF] + dot_t(bas[i], lfield[i].astype(BF16))

    def near_step(k, _):
        near_leaf(2 * k)
        near_leaf(2 * k + 1)
        return 0

    lax.fori_loop(0, OWN // 2, near_step, 0)

    def drain(i, _):
        give_copy(i).wait()
        return 0

    lax.fori_loop(0, OWN, drain, 0)
    to_sibling.wait_send()
    for one in to_after + to_before + fwd_low + fwd_high + coef_out + ring_up + ring_down + [cross] + fields_out:
        one.wait_send()
    for n in range(4):
        if_not(r == n + 1, n < 2, sums_out[n].wait_send)
    for n in range(8):
        if_not(odd == 0, n == 0, to_peers[n].wait_send)


def shards(
    sources, near_tiles, near_index, near_count, leaf_basis, leaf_coupling, leaf_far, up_leaf, mid_coupling, mid_far,
    up_mid, top_coupling,
):
    hbm_spec = pl.BlockSpec(memory_space=pltpu.MemorySpace.HBM)
    vmem_spec = pl.BlockSpec(memory_space=pltpu.MemorySpace.VMEM)
    dma, vmem, smem = pltpu.SemaphoreType.DMA, pltpu.VMEM, pltpu.SMEM
    operands = [
        sources.reshape(OWN, LEAF, HALF), near_tiles, near_index.T, near_count, leaf_basis, leaf_coupling, leaf_far.T,
        up_leaf, mid_coupling, mid_far, up_mid, top_coupling,
    ]
    near, take = pl.pallas_call(
        kernel,
        out_shape=(
            jax.ShapeDtypeStruct((OWN, LEAF, HALF), F32),
            jax.ShapeDtypeStruct((OWN, LEAF, HALF), BF16),
        ),
        in_specs=[hbm_spec] * 12,
        out_specs=(vmem_spec, vmem_spec),
        scratch_shapes=[
            smem((2 * SLOTS, OWN), jnp.int32), smem((OWN,), jnp.int32),
            smem((4, OWN), jnp.int32), smem((MIDS, 4), jnp.int32),
            vmem((WINDOW + 1, LEAF, HALF), BF16),
            vmem((WINDOW + 1, LEAF, HALF), BF16),
            vmem((OWN, SLOTS, LEAF, LEAF), BF16),
            vmem((OWN, RANK, LEAF), BF16),
            vmem((OWN, RANK, 4 * RANK), BF16),
            vmem((MIDS, RANK, 8 * RANK), BF16),
            vmem((MIDS, RANK, 4 * RANK), BF16),
            vmem((MIDS, RANK, RANK), BF16),
            vmem((8, RANK, 2 * RANK), BF16),
            vmem((WINDOW, RANK, HALF), BF16),
            vmem((MID_WINDOW, RANK, HALF), BF16),
            vmem((RANK, HALF), BF16),
            vmem((GROUP, RANK, HALF), BF16),
            vmem((RANK, HALF), BF16),
            vmem((8, 2, RANK, HALF), BF16),
            vmem((RANK, HALF), BF16),
            vmem((3, RANK, HALF), BF16),
            vmem((OWN, RANK, HALF), F32),
            vmem((OWN, LEAF, HALF), BF16),
            dma((18,)), dma((4,)),
            dma(()), dma(()),
            dma((2, CHUNKS)), dma((2, CHUNKS)),
            dma((2, CHUNKS)), dma((2, CHUNKS)),
            dma((2,)), dma((2,)),
            dma((2, 4)), dma((2, 4)),
            dma((4,)), dma((GROUP,)),
            dma((8,)), dma((8,)),
            dma((3,)), dma((3,)),
            dma((OWN,)), dma((OWN,)),
        ],
        compiler_params=pltpu.CompilerParams(
            collective_id=0, has_side_effects=True, vmem_limit_bytes=48 * 2**20
        ),
        name="h2_product",
    )(*[pltpu.with_memory_space_constraint(v, pltpu.MemorySpace.HBM) for v in operands])
    return (near + take.astype(F32)).reshape(OWN * LEAF, HALF)


def solution(mesh):
    return jax.shard_map(
        shards,
        mesh=mesh,
        in_specs=(
            P("leaf", "col"),
            P("leaf", "col", None, None),
            P("leaf", None),
            P("leaf"),
            P("leaf", None, None),
            P("leaf", None, None),
            P("leaf", None),
            P("leaf", None, None),
            P("leaf", None, None),
            P("leaf", None),
            P("leaf", None, None),
            P(),
        ),
        out_specs=P("leaf", "col"),
        check_vma=False,
    )
```

```python
import functools

import jax
import jax.numpy as jnp
from jax import lax
from jax.experimental import pallas as pl
from jax.experimental.pallas import tpu as pltpu
from jax.sharding import PartitionSpec as P

MESH = pl.DeviceIdType.MESH
F32 = jnp.float32
BF16 = jnp.bfloat16

LEAF = 256
RANK = 64
HALF = 128
OWN = 16
HALO = 8
MIDS = 2
GROUP = 4
RING = 8
COLUMNS = 16
SLOTS = 4
WINDOW = OWN + 2 * HALO
CHUNKS = (4, 2, 2)
MID_WINDOW = 4 * GROUP * MIDS


def dot(a, b):
    return jnp.dot(a, b, preferred_element_type=F32)


def by_fours(body):
    def step(k, _):
        for i in range(4):
            body(4 * k + i)
        return 0

    lax.fori_loop(0, OWN // 4, step, 0)


def kernel(
    src, tiles, near_index_in, near_count_in, basis, coupling, leaf_far_in, up_leaf, mid_coupling, mid_far_in, up_mid,
    top_coupling,
    near, take,
    near_index, near_count, leaf_far, mid_far,
    own0, own1, ha0, ha1, hb0, hb1, hc0, hc1, tile, bas, cpl, upl, mcp, upm, bat, upl_t, upm_t, top, coef, mid, part, top_a, coef_top, top_b, field, top_c, lfield, give,
    load_sem, tile_sem, sib_send, sib_recv, halo_send, halo_recv, fwd_send, fwd_recv, coef_send, coef_recv,
    mid_send, mid_recv, cross_send, cross_recv, a_send, a_recv, b_send, b_recv, c_send, c_recv, give_send, give_recv,
):
    d, c = lax.axis_index("leaf"), lax.axis_index("col")
    devices = COLUMNS * RING
    g, r = d // GROUP, d % GROUP
    column, z = d // RING, d % RING
    half, x, y = g % 2, column % 4, column // 4
    sibling = (d, 1 - c)
    after, before = ((d + 1) % devices, c), ((d + devices - 1) % devices, c)
    mates = [(g * GROUP + (r + o) % GROUP, c) for o in (1, 2, 3)]
    inner = (r * (3 - r)) // 2
    other = column * RING + (1 - half) * GROUP
    sums = [(g * GROUP + 1, c), (g * GROUP + 2, c), (other, c), (other + 3, c)]
    sum_of = inner * half + (1 - inner) * (1 - half)
    odd = r // 2
    peers = [
        (((((y + 2 * jj + odd) % 4) * 4 + (x + xo) % 4) * RING + z), jj, xo) for jj in range(2) for xo in range(4)
    ]
    across = (((column + 1 - 2 * half + COLUMNS) % COLUMNS) * RING + z, c)
    across_from = (((column - 1 + 2 * half + COLUMNS) % COLUMNS) * RING + z, c)

    def copy(a, b, send, recv, device):
        return pltpu.make_async_remote_copy(
            src_ref=a, dst_ref=b, send_sem=send, recv_sem=recv, device_id=device, device_id_type=MESH
        )

    def if_not(flag, here, body):
        if here:
            pl.when(jnp.logical_not(flag))(body)
        else:
            body()

    barrier = pltpu.get_barrier_semaphore()

    def greet(device):
        pl.semaphore_signal(barrier, inc=1, device_id=device, device_id_type=MESH)

    column_mates = [(column * RING + (z + o) % RING, c) for o in range(1, RING)]
    for device in [sibling, after, before, across, across_from] + column_mates:
        greet(device)
    for device, jj, xo in peers:
        if_not(odd == 0, jj == 0 and xo == 0, functools.partial(greet, (device, c)))

    loads = [
        pltpu.make_async_copy(src, own0.at[pl.ds(0, OWN)], load_sem.at[0]),
        pltpu.make_async_copy(basis, bas, load_sem.at[1]),
        pltpu.make_async_copy(up_leaf, upl, load_sem.at[2]),
        pltpu.make_async_copy(up_mid, upm, load_sem.at[3]),
        pltpu.make_async_copy(leaf_far_in, leaf_far, load_sem.at[4]),
        pltpu.make_async_copy(mid_far_in, mid_far, load_sem.at[5]),
        pltpu.make_async_copy(near_index_in, near_index, load_sem.at[6]),
        pltpu.make_async_copy(near_count_in, near_count, load_sem.at[7]),
        pltpu.make_async_copy(coupling, cpl, load_sem.at[8]),
        pltpu.make_async_copy(mid_coupling, mcp, load_sem.at[9]),
    ]
    for device, jj, xo in peers:
        pair = ((y + 2 * jj + odd) % 4) * 4 + (x + xo) % 4
        loads.append(
            pltpu.make_async_copy(
                top_coupling.at[g, :, pl.ds(pl.multiple_of(pair * 2 * RANK, 2 * RANK), 2 * RANK)],
                top.at[4 * jj + xo],
                load_sem.at[10 + 4 * jj + xo],
            )
        )
    for load in loads:
        load.start()
    tile_loads = [
        pltpu.make_async_copy(tiles.at[pl.ds(4 * k, 4)], tile.at[pl.ds(4 * k, 4)], tile_sem.at[k]) for k in range(4)
    ]
    for load in tile_loads:
        load.start()

    zero = jnp.zeros((LEAF, HALF), BF16)
    own0[OWN] = zero
    own1[OWN] = zero
    for n in range(8):
        top_b[n, 1 - sum_of] = jnp.zeros((RANK, HALF), BF16)

    @pl.when(odd == 0)
    def _():
        top_b[0, sum_of] = jnp.zeros((RANK, HALF), BF16)
        pl.semaphore_wait(barrier, 19)

    @pl.when(odd != 0)
    def _():
        pl.semaphore_wait(barrier, 20)

    to_sibling = copy(src, own1.at[pl.ds(0, OWN)], sib_send, sib_recv, sibling)
    halos, forwards = [], []
    done = 0
    for i, (h0, h1) in enumerate(((ha0, ha1), (hb0, hb1), (hc0, hc1))):
        n = CHUNKS[i]
        halos.append(
            (
                copy(src.at[pl.ds(OWN - done - n, n)], h0.at[0], halo_send.at[0, i], halo_recv.at[0, i], after),
                copy(src.at[pl.ds(done, n)], h0.at[1], halo_send.at[1, i], halo_recv.at[1, i], before),
            )
        )
        forwards.append(copy(h0, h1, fwd_send.at[i], fwd_recv.at[i], sibling))
        done += n

    def forward(i):
        for one in halos[i]:
            one.wait_recv()
        forwards[i].start()

    for one in halos[0]:
        one.start()
    to_sibling.start()

    loads[0].wait()
    loads[1].wait()

    def leaf_step(i):
        coef[HALO + i] = dot(bas[i], own0[i]).astype(BF16)

    by_fours(leaf_step)
    coef_out = [
        copy(coef.at[pl.ds(OWN, HALO)], coef.at[pl.ds(0, HALO)], coef_send.at[0], coef_recv.at[0], after),
        copy(coef.at[pl.ds(HALO, HALO)], coef.at[pl.ds(HALO + OWN, HALO)], coef_send.at[1], coef_recv.at[1], before),
    ]

    loads[2].wait()
    loads[3].wait()
    base = GROUP * MIDS
    values = [
        dot(upl[q], coef[pl.ds(HALO + 8 * q, 8)].reshape(8 * RANK, HALF)).astype(BF16) for q in range(MIDS)
    ]
    lifts = [dot(upm[q], values[q]).astype(BF16).astype(F32) for q in range(MIDS)]
    part[...] = (lifts[0] + lifts[1]).astype(BF16)
    for q in range(MIDS):
        mid[base + MIDS * z + q] = values[q]
    sums_out = [copy(part, top_a.at[r], a_send.at[n], a_recv.at[r], sums[n]) for n in range(4)]
    for n in range(4):
        if_not(r == n + 1, n < 2, sums_out[n].start)

    def near_z(o):
        return (column * RING + (z + o + RING) % RING, c)

    def of(o):
        return mid.at[pl.ds(base + MIDS * ((z + o + RING) % RING), MIDS)]

    up = 1 - 2 * c
    steps = [(0, 1), (0, -1), (0, 2), (0, -2), (-2, 1), (2, -1), (-2 * up, 2 * up)]
    mid_out = [
        copy(of(whose), of(whose), mid_send.at[n], mid_recv.at[n], near_z(o)) for n, (whose, o) in enumerate(steps)
    ]
    mid_got = [
        copy(of(whose - o), of(whose - o), mid_send.at[n], mid_recv.at[n], near_z(o))
        for n, (whose, o) in enumerate(steps)
    ]

    def cross(o):
        member = (z + o + RING) % GROUP
        there = mid.at[pl.ds(3 * base * half + MIDS * member, MIDS)]
        return copy(of(o), there, cross_send.at[member], cross_recv.at[member], across)

    def send_across(offsets):
        for o in offsets:
            pl.when(((z + o + RING) % RING) // GROUP != half)(cross(o).start)

    for n in range(4):
        mid_out[n].start()
    for one in coef_out:
        one.start()

    for n in range(GROUP):
        got = copy(part, top_a.at[n], a_send.at[0], a_recv.at[n], sibling)
        pl.when(jnp.logical_or(inner == 0, r != n))(got.wait_recv)

    @pl.when(inner == 1)
    def _():
        top_a[r] = part[...]

    total = (top_a[0].astype(F32) + top_a[1].astype(F32)) + (top_a[2].astype(F32) + top_a[3].astype(F32))
    coef_top[...] = total.astype(BF16)
    to_peers = []
    for device, jj, xo in peers:
        slot = 4 * ((jj + odd) % 2) + (4 - xo) % 4
        one = copy(coef_top, top_b.at[slot, sum_of], b_send.at[4 * jj + xo], b_recv.at[slot], (device, c))
        to_peers.append(one)
        if_not(odd == 0, jj == 0 and xo == 0, one.start)

    for one in halos[1]:
        one.start()

    @pl.when(r == 0)
    def _():
        top_b[0, sum_of] = coef_top[...]

    for n in (2, 3):
        mid_got[n].wait_recv()
    for n in (4, 5, 6):
        mid_out[n].start()
    for n in (0, 1):
        mid_got[n].wait_recv()
    send_across((1, -1, 2, -2))

    def turn(i):
        bat[i] = bas[i].T

    by_fours(turn)
    for q in range(MIDS):
        upl_t[q] = upl[q].T
        upm_t[q] = upm[q].T
    loads[4].wait()
    loads[8].wait()
    for one in coef_out:
        one.wait_recv()

    def far_step(i):
        picked = [coef[jnp.clip(leaf_far[f, i] - (d * OWN - HALO), 0, WINDOW - 1)] for f in range(4)]
        lfield[i] = dot(cpl[i], jnp.concatenate(picked, axis=0))

    by_fours(far_step)

    for n in range(8):
        loads[10 + n].wait()
    for n in range(8):
        got = copy(coef_top, top_b.at[n, sum_of], b_send.at[n], b_recv.at[n], sibling)
        if_not(odd == 0, n == 0, got.wait_recv)
    terms = [dot(top[n], top_b[n].reshape(2 * RANK, HALF)) for n in range(8)]
    total = ((terms[0] + terms[1]) + (terms[2] + terms[3])) + ((terms[4] + terms[5]) + (terms[6] + terms[7]))
    field[...] = total.astype(BF16)
    fields_out = [copy(field, top_c.at[o], c_send.at[o], c_recv.at[o], mates[o]) for o in range(3)]
    for one in fields_out:
        one.start()
    for one in halos[2]:
        one.start()
    for n in (4, 5, 6):
        mid_got[n].wait_recv()
    send_across((3, -3, 4))

    reach = [(ha0, ha1, 4, 20), (hb0, hb1, 2, 26), (hc0, hc1, 0, 30)]
    batches = [(4, 4, 4), (2, 10, 2), (0, 14, 2)]

    def give_copy(phase, k):
        first, step, n = batches[phase]
        here = pl.ds(first + step * k, n)
        return copy(give.at[here], take.at[here], give_send.at[phase, k], give_recv.at[phase, k], sibling)

    def near_rows(i, s, k, phase):
        slot = c * SLOTS + s
        j = near_index[slot, i] - (d * OWN - HALO)
        live = slot < near_count[i]
        inside = jnp.logical_and(live, jnp.logical_and(j >= HALO, j < HALO + OWN))
        m = jnp.where(inside, jnp.clip(j - HALO, 0, OWN - 1), OWN)
        low, high = own0[m], own1[m]
        for p in range(phase + 1):
            h0, h1, first, step = reach[p]
            m = j - (first + step * k)
            inside = jnp.logical_and(live, jnp.logical_and(m >= 0, m < CHUNKS[p]))
            m = jnp.clip(m, 0, CHUNKS[p] - 1)
            low, high = jnp.where(inside, h0[k, m], low), jnp.where(inside, h1[k, m], high)
        return jnp.concatenate([low, high], axis=1)

    def near_phase(phase, fresh=False):
        forwards[phase].wait_recv()
        first, step, n = batches[phase]

        def side(k, _):
            for i in range(n):
                leaf = first + step * k + i
                terms = [dot(tile[leaf, s], near_rows(leaf, s, k, phase)) for s in range(SLOTS)]
                total = (terms[0] + terms[1]) + (terms[2] + terms[3])
                give[leaf] = total[:, HALF:].astype(BF16)
                near[leaf] = total[:, :HALF] if fresh else near[leaf] + total[:, :HALF]
            give_copy(phase, k).start()
            return 0

        lax.fori_loop(0, 2, side, 0)

    loads[6].wait()
    loads[7].wait()
    to_sibling.wait_recv()
    for load in tile_loads:
        load.wait()

    forward(0)
    near_phase(0, True)
    for one in fields_out:
        one.wait_recv()
    top_field = ((total + top_c[0].astype(F32)) + (top_c[1].astype(F32) + top_c[2].astype(F32))).astype(BF16)
    lifted = [dot(upm_t[q], top_field) for q in range(MIDS)]

    loads[5].wait()
    loads[9].wait()
    for n in range(GROUP):
        got = mid.at[pl.ds(3 * base * half + MIDS * n, MIDS)]
        copy(got, got, cross_send.at[n], cross_recv.at[n], across).wait_recv()
    first = column * RING * MIDS - base
    for q in range(MIDS):
        picked = [mid[jnp.clip(mid_far[q, f] - first, 0, MID_WINDOW - 1)] for f in range(4)]
        value = (dot(mcp[q], jnp.concatenate(picked, axis=0)) + lifted[q]).astype(BF16)
        down = dot(upl_t[q], value).reshape(8, RANK, HALF)
        lfield[pl.ds(8 * q, 8)] = lfield[pl.ds(8 * q, 8)] + down

    def product_step(k, _):
        for i in range(4):
            inner_leaf, outer_leaf = 4 + 4 * k + i, 12 * k + i
            near[inner_leaf] = near[inner_leaf] + dot(bat[inner_leaf], lfield[inner_leaf].astype(BF16))
            near[outer_leaf] = dot(bat[outer_leaf], lfield[outer_leaf].astype(BF16))
        return 0

    lax.fori_loop(0, 2, product_step, 0)

    forward(1)
    forward(2)
    near_phase(1)
    near_phase(2)

    for phase in range(3):
        for k in range(2):
            give_copy(phase, k).wait()
    to_sibling.wait_send()
    for one in [one for pair in halos for one in pair] + forwards + coef_out + mid_out + fields_out:
        one.wait_send()
    for n in range(GROUP):
        if_not(r == n + 1, n < 2, sums_out[n].wait_send)
        cross(4 - r + n).wait_send()
    for n in range(8):
        if_not(odd == 0, n == 0, to_peers[n].wait_send)


def shards(
    sources, near_tiles, near_index, near_count, leaf_basis, leaf_coupling, leaf_far, up_leaf, mid_coupling, mid_far,
    up_mid, top_coupling,
):
    hbm_spec = pl.BlockSpec(memory_space=pltpu.MemorySpace.HBM)
    vmem_spec = pl.BlockSpec(memory_space=pltpu.MemorySpace.VMEM)
    dma, vmem, smem = pltpu.SemaphoreType.DMA, pltpu.VMEM, pltpu.SMEM
    operands = [
        sources.reshape(OWN, LEAF, HALF), near_tiles, near_index.T, near_count, leaf_basis, leaf_coupling, leaf_far.T,
        up_leaf, mid_coupling, mid_far, up_mid, top_coupling,
    ]
    near, take = pl.pallas_call(
        kernel,
        out_shape=(
            jax.ShapeDtypeStruct((OWN, LEAF, HALF), F32),
            jax.ShapeDtypeStruct((OWN, LEAF, HALF), BF16),
        ),
        in_specs=[hbm_spec] * 12,
        out_specs=(vmem_spec, vmem_spec),
        scratch_shapes=[
            smem((2 * SLOTS, OWN), jnp.int32), smem((OWN,), jnp.int32),
            smem((4, OWN), jnp.int32), smem((MIDS, 4), jnp.int32),
            vmem((OWN + 1, LEAF, HALF), BF16),
            vmem((OWN + 1, LEAF, HALF), BF16),
            *[vmem((2, n, LEAF, HALF), BF16) for n in CHUNKS for _ in range(2)],
            vmem((OWN, SLOTS, LEAF, LEAF), BF16),
            vmem((OWN, RANK, LEAF), BF16),
            vmem((OWN, RANK, 4 * RANK), BF16),
            vmem((MIDS, RANK, 8 * RANK), BF16),
            vmem((MIDS, RANK, 4 * RANK), BF16),
            vmem((MIDS, RANK, RANK), BF16),
            vmem((OWN, LEAF, RANK), BF16),
            vmem((MIDS, 8 * RANK, RANK), BF16),
            vmem((MIDS, RANK, RANK), BF16),
            vmem((8, RANK, 2 * RANK), BF16),
            vmem((WINDOW, RANK, HALF), BF16),
            vmem((MID_WINDOW, RANK, HALF), BF16),
            vmem((RANK, HALF), BF16),
            vmem((GROUP, RANK, HALF), BF16),
            vmem((RANK, HALF), BF16),
            vmem((8, 2, RANK, HALF), BF16),
            vmem((RANK, HALF), BF16),
            vmem((3, RANK, HALF), BF16),
            vmem((OWN, RANK, HALF), F32),
            vmem((OWN, LEAF, HALF), BF16),
            dma((18,)), dma((4,)),
            dma(()), dma(()),
            dma((2, 3)), dma((2, 3)),
            dma((3,)), dma((3,)),
            dma((2,)), dma((2,)),
            dma((7,)), dma((7,)),
            dma((GROUP,)), dma((GROUP,)),
            dma((4,)), dma((GROUP,)),
            dma((8,)), dma((8,)),
            dma((3,)), dma((3,)),
            dma((3, 2)), dma((3, 2)),
        ],
        compiler_params=pltpu.CompilerParams(
            collective_id=0, has_side_effects=True, vmem_limit_bytes=48 * 2**20
        ),
        name="h2_product",
    )(*[pltpu.with_memory_space_constraint(v, pltpu.MemorySpace.HBM) for v in operands])
    return (near + take.astype(F32)).reshape(OWN * LEAF, HALF)


def solution(mesh):
    return jax.shard_map(
        shards,
        mesh=mesh,
        in_specs=(
            P("leaf", "col"),
            P("leaf", "col", None, None),
            P("leaf", None),
            P("leaf"),
            P("leaf", None, None),
            P("leaf", None, None),
            P("leaf", None),
            P("leaf", None, None),
            P("leaf", None, None),
            P("leaf", None),
            P("leaf", None, None),
            P(),
        ),
        out_specs=P("leaf", "col"),
        check_vma=False,
    )
```

```python
import jax
import jax.numpy as jnp
from jax import lax
from jax.experimental import pallas as pl
from jax.experimental.pallas import tpu as pltpu
from jax.sharding import PartitionSpec as P

MESH = pl.DeviceIdType.MESH
F32 = jnp.float32
BF16 = jnp.bfloat16

LEAF = 256
RANK = 64
HALF = 128
OWN = 16
HALO = 8
MIDS = 2
GROUP = 4
RING = 8
COLUMNS = 16
SLOTS = 4
WINDOW = OWN + 2 * HALO
CHUNKS = (2, 2, 2, 2)
TOP_WIDTH = 2 * COLUMNS * RANK
ROWS = 2 * RANK // RING
MID_WINDOW = 4 * GROUP * MIDS


def dot(a, b):
    return jnp.dot(a, b, preferred_element_type=F32)


def by_fours(body):
    def step(k, _):
        for i in range(4):
            body(4 * k + i)
        return 0

    lax.fori_loop(0, OWN // 4, step, 0)


def kernel(
    src, tiles, near_index_in, near_count_in, basis, coupling, leaf_far_in, up_leaf, mid_coupling, mid_far_in, up_mid,
    top_coupling,
    near, take,
    near_index, near_count, leaf_far, mid_far,
    own0, own1, ha0, ha1, hb0, hb1, hc0, hc1, hd0, hd1, tile, bas, cpl, upl, mcp, upm, bat, upl_t, upm_t, top, coef, mid, part, top_b, field, top_c, rows, lfield, give,
    load_sem, tile_sem, sib_send, sib_recv, halo_send, halo_recv, fwd_send, fwd_recv, coef_send, coef_recv,
    mid_send, mid_recv, cross_send, cross_recv, b_send, b_recv, c_send, c_recv, d_send, d_recv, give_send, give_recv,
):
    d, c = lax.axis_index("leaf"), lax.axis_index("col")
    devices = COLUMNS * RING
    g, r = d // GROUP, d % GROUP
    column, z = d // RING, d % RING
    half, x, y = g % 2, column % 4, column // 4
    sibling = (d, 1 - c)
    after, before = ((d + 1) % devices, c), ((d + devices - 1) % devices, c)
    mates = [(g * GROUP + (r + o) % GROUP, c) for o in (1, 2, 3)]
    offsets = [(yo, xo) for yo in range(4) for xo in range(4) if yo or xo]
    peers = [((((y + yo) % 4) * 4 + (x + xo) % 4) * RING + z, c) for yo, xo in offsets]
    across = (((column + 1 - 2 * half + COLUMNS) % COLUMNS) * RING + z, c)
    across_from = (((column - 1 + 2 * half + COLUMNS) % COLUMNS) * RING + z, c)

    def copy(a, b, send, recv, device):
        return pltpu.make_async_remote_copy(
            src_ref=a, dst_ref=b, send_sem=send, recv_sem=recv, device_id=device, device_id_type=MESH
        )

    barrier = pltpu.get_barrier_semaphore()

    def greet(device):
        pl.semaphore_signal(barrier, inc=1, device_id=device, device_id_type=MESH)

    column_mates = [(column * RING + (z + o) % RING, c) for o in range(1, RING)]
    greeted = [sibling, after, before, across, across_from] + column_mates + peers
    for device in greeted:
        greet(device)

    loads = [
        pltpu.make_async_copy(src, own0.at[pl.ds(0, OWN)], load_sem.at[0]),
        pltpu.make_async_copy(basis, bas, load_sem.at[1]),
        pltpu.make_async_copy(up_leaf, upl, load_sem.at[2]),
        pltpu.make_async_copy(up_mid, upm, load_sem.at[3]),
        pltpu.make_async_copy(leaf_far_in, leaf_far, load_sem.at[4]),
        pltpu.make_async_copy(mid_far_in, mid_far, load_sem.at[5]),
        pltpu.make_async_copy(near_index_in, near_index, load_sem.at[6]),
        pltpu.make_async_copy(near_count_in, near_count, load_sem.at[7]),
        pltpu.make_async_copy(coupling, cpl, load_sem.at[8]),
        pltpu.make_async_copy(mid_coupling, mcp, load_sem.at[9]),
    ]
    loads.append(pltpu.make_async_copy(top_coupling.at[pl.ds(2 * column, 2)], top, load_sem.at[10]))
    for load in loads:
        load.start()
    tile_loads = [
        pltpu.make_async_copy(tiles.at[pl.ds(4 * k, 4)], tile.at[pl.ds(4 * k, 4)], tile_sem.at[k]) for k in range(4)
    ]
    for load in tile_loads:
        load.start()

    zero = jnp.zeros((LEAF, HALF), BF16)
    own0[OWN] = zero
    own1[OWN] = zero
    for n in range(COLUMNS):
        top_b[n, 1 - half] = jnp.zeros((RANK, HALF), BF16)
    pl.semaphore_wait(barrier, len(greeted))

    to_sibling = copy(src, own1.at[pl.ds(0, OWN)], sib_send, sib_recv, sibling)
    halos, forwards = [], []
    done = 0
    for i, (h0, h1) in enumerate(((ha0, ha1), (hb0, hb1), (hc0, hc1), (hd0, hd1))):
        n = CHUNKS[i]
        halos.append(
            (
                copy(src.at[pl.ds(OWN - done - n, n)], h0.at[0], halo_send.at[0, i], halo_recv.at[0, i], after),
                copy(src.at[pl.ds(done, n)], h0.at[1], halo_send.at[1, i], halo_recv.at[1, i], before),
            )
        )
        forwards.append(copy(h0, h1, fwd_send.at[i], fwd_recv.at[i], sibling))
        done += n

    def forward(i):
        for one in halos[i]:
            one.wait_recv()
        forwards[i].start()

    for one in halos[0]:
        one.start()
    to_sibling.start()

    loads[0].wait()
    loads[1].wait()

    def leaf_step(i):
        coef[HALO + i] = dot(bas[i], own0[i]).astype(BF16)

    by_fours(leaf_step)
    coef_out = [
        copy(coef.at[pl.ds(OWN, HALO)], coef.at[pl.ds(0, HALO)], coef_send.at[0], coef_recv.at[0], after),
        copy(coef.at[pl.ds(HALO, HALO)], coef.at[pl.ds(HALO + OWN, HALO)], coef_send.at[1], coef_recv.at[1], before),
    ]

    loads[2].wait()
    loads[3].wait()
    base = GROUP * MIDS
    values = [
        dot(upl[q], coef[pl.ds(HALO + 8 * q, 8)].reshape(8 * RANK, HALF)).astype(BF16) for q in range(MIDS)
    ]
    lifts = [dot(upm[q], values[q]).astype(BF16).astype(F32) for q in range(MIDS)]
    part[...] = (lifts[0] + lifts[1]).astype(BF16)
    for q in range(MIDS):
        mid[base + MIDS * z + q] = values[q]

    to_peers = []
    for n, (yo, xo) in enumerate(offsets):
        back = offsets.index(((4 - yo) % 4, (4 - xo) % 4))
        to_peers.append(copy(part, top_b.at[column, half], b_send.at[n], b_recv.at[back], peers[n]))

    def near_z(o):
        return (column * RING + (z + o + RING) % RING, c)

    def of(o):
        return mid.at[pl.ds(base + MIDS * ((z + o + RING) % RING), MIDS)]

    up = 1 - 2 * c
    steps = [(0, 1), (0, -1), (0, 2), (0, -2), (-2, 1), (2, -1), (-2 * up, 2 * up)]
    mid_out = [
        copy(of(whose), of(whose), mid_send.at[n], mid_recv.at[n], near_z(o)) for n, (whose, o) in enumerate(steps)
    ]
    mid_got = [
        copy(of(whose - o), of(whose - o), mid_send.at[n], mid_recv.at[n], near_z(o))
        for n, (whose, o) in enumerate(steps)
    ]

    def cross(o):
        member = (z + o + RING) % GROUP
        there = mid.at[pl.ds(3 * base * half + MIDS * member, MIDS)]
        return copy(of(o), there, cross_send.at[member], cross_recv.at[member], across)

    def send_across(offsets):
        for o in offsets:
            pl.when(((z + o + RING) % RING) // GROUP != half)(cross(o).start)

    for n in range(4):
        mid_out[n].start()
    for one in to_peers:
        one.start()
    for one in coef_out:
        one.start()
    top_b[column, half] = part[...]

    for one in halos[1]:
        one.start()
    for n in (2, 3):
        mid_got[n].wait_recv()
    for n in (4, 5, 6):
        mid_out[n].start()
    for n in (0, 1):
        mid_got[n].wait_recv()
    send_across((1, -1, 2, -2))

    def turn(i):
        bat[i] = bas[i].T

    by_fours(turn)
    for q in range(MIDS):
        upl_t[q] = upl[q].T
        upm_t[q] = upm[q].T
    loads[4].wait()
    loads[8].wait()
    for one in coef_out:
        one.wait_recv()

    def far_step(i):
        picked = [coef[jnp.clip(leaf_far[f, i] - (d * OWN - HALO), 0, WINDOW - 1)] for f in range(4)]
        lfield[i] = dot(cpl[i], jnp.concatenate(picked, axis=0))

    by_fours(far_step)

    loads[10].wait()
    lanes = pl.ds(pl.multiple_of(column * 2 * RANK, 2 * RANK), 2 * RANK)
    itself = lax.broadcasted_iota(jnp.int32, (RANK, 2 * RANK), 1) // RANK == half
    top[half, :, lanes] = jnp.where(itself, 0.0, top[half, :, lanes].astype(F32)).astype(BF16)

    for n in range(len(peers)):
        yo, xo = offsets[n]
        from_column = ((y + yo) % 4) * 4 + (x + xo) % 4
        copy(part, top_b.at[from_column, half], b_send.at[n], b_recv.at[n], sibling).wait_recv()
    total = dot(top[...].reshape(2 * RANK, TOP_WIDTH), top_b[...].reshape(TOP_WIDTH, HALF))
    field[...] = total.astype(BF16).reshape(RING, ROWS, HALF)
    fields_out = []
    for o in range(1, RING):
        there = (z + o) % RING
        fields_out.append(
            copy(field.at[there], top_c.at[o], c_send.at[o - 1], c_recv.at[o - 1], column_mates[o - 1])
        )
    for one in fields_out:
        one.start()
    for one in halos[2]:
        one.start()
    for n in (4, 5, 6):
        mid_got[n].wait_recv()
    send_across((3, -3, 4))
    for one in fields_out:
        one.wait_recv()
    reduced = field[z].astype(F32)
    for o in range(1, RING):
        reduced = reduced + top_c[o].astype(F32)
    rows[r] = reduced.astype(BF16)
    rows_out = [copy(rows.at[r], rows.at[r], d_send.at[o], d_recv.at[o], mates[o]) for o in range(3)]
    for one in rows_out:
        one.start()
    for one in halos[3]:
        one.start()

    reach = [(ha0, ha1, 6, 18), (hb0, hb1, 4, 22), (hc0, hc1, 2, 26), (hd0, hd1, 0, 30)]
    batches = [(6, 2, 2), (4, 6, 2), (2, 10, 2), (0, 14, 2)]

    def give_copy(phase, k):
        first, step, n = batches[phase]
        here = pl.ds(first + step * k, n)
        return copy(give.at[here], take.at[here], give_send.at[phase, k], give_recv.at[phase, k], sibling)

    def near_rows(i, s, k, phase):
        slot = c * SLOTS + s
        j = near_index[slot, i] - (d * OWN - HALO)
        live = slot < near_count[i]
        inside = jnp.logical_and(live, jnp.logical_and(j >= HALO, j < HALO + OWN))
        m = jnp.where(inside, jnp.clip(j - HALO, 0, OWN - 1), OWN)
        low, high = own0[m], own1[m]
        for p in range(phase + 1):
            h0, h1, first, step = reach[p]
            m = j - (first + step * k)
            inside = jnp.logical_and(live, jnp.logical_and(m >= 0, m < CHUNKS[p]))
            m = jnp.clip(m, 0, CHUNKS[p] - 1)
            low, high = jnp.where(inside, h0[k, m], low), jnp.where(inside, h1[k, m], high)
        return jnp.concatenate([low, high], axis=1)

    def near_phase(phase, fresh=False):
        forwards[phase].wait_recv()
        first, step, n = batches[phase]

        def side(k, _):
            for i in range(n):
                leaf = first + step * k + i
                terms = [dot(tile[leaf, s], near_rows(leaf, s, k, phase)) for s in range(SLOTS)]
                total = (terms[0] + terms[1]) + (terms[2] + terms[3])
                give[leaf] = total[:, HALF:].astype(BF16)
                near[leaf] = total[:, :HALF] if fresh else near[leaf] + total[:, :HALF]
            give_copy(phase, k).start()
            return 0

        lax.fori_loop(0, 2, side, 0)

    loads[6].wait()
    loads[7].wait()
    to_sibling.wait_recv()
    for load in tile_loads:
        load.wait()

    forward(0)
    forward(1)
    near_phase(0, True)
    near_phase(1, True)
    for n in range(3):
        got = rows.at[(r + 3 - n) % GROUP]
        copy(got, got, d_send.at[n], d_recv.at[n], sibling).wait_recv()
    top_field = rows[...].reshape(RANK, HALF)
    lifted = [dot(upm_t[q], top_field) for q in range(MIDS)]

    loads[5].wait()
    loads[9].wait()
    for n in range(GROUP):
        got = mid.at[pl.ds(3 * base * half + MIDS * n, MIDS)]
        copy(got, got, cross_send.at[n], cross_recv.at[n], across).wait_recv()
    first = column * RING * MIDS - base
    for q in range(MIDS):
        picked = [mid[jnp.clip(mid_far[q, f] - first, 0, MID_WINDOW - 1)] for f in range(4)]
        value = (dot(mcp[q], jnp.concatenate(picked, axis=0)) + lifted[q]).astype(BF16)
        down = dot(upl_t[q], value).reshape(8, RANK, HALF)
        lfield[pl.ds(8 * q, 8)] = lfield[pl.ds(8 * q, 8)] + down

    def product_step(k, _):
        for i in range(4):
            inner_leaf, outer_leaf = 4 + 4 * k + i, 12 * k + i
            near[inner_leaf] = near[inner_leaf] + dot(bat[inner_leaf], lfield[inner_leaf].astype(BF16))
            near[outer_leaf] = dot(bat[outer_leaf], lfield[outer_leaf].astype(BF16))
        return 0

    lax.fori_loop(0, 2, product_step, 0)

    forward(2)
    forward(3)
    near_phase(2)
    near_phase(3)

    for phase in range(4):
        for k in range(2):
            give_copy(phase, k).wait()
    to_sibling.wait_send()
    for one in [one for pair in halos for one in pair] + forwards + coef_out + mid_out + to_peers + fields_out + rows_out:
        one.wait_send()
    for n in range(GROUP):
        cross(4 - r + n).wait_send()


def shards(
    sources, near_tiles, near_index, near_count, leaf_basis, leaf_coupling, leaf_far, up_leaf, mid_coupling, mid_far,
    up_mid, top_coupling,
):
    hbm_spec = pl.BlockSpec(memory_space=pltpu.MemorySpace.HBM)
    vmem_spec = pl.BlockSpec(memory_space=pltpu.MemorySpace.VMEM)
    dma, vmem, smem = pltpu.SemaphoreType.DMA, pltpu.VMEM, pltpu.SMEM
    operands = [
        sources.reshape(OWN, LEAF, HALF), near_tiles, near_index.T, near_count, leaf_basis, leaf_coupling, leaf_far.T,
        up_leaf, mid_coupling, mid_far, up_mid, top_coupling,
    ]
    near, take = pl.pallas_call(
        kernel,
        out_shape=(
            jax.ShapeDtypeStruct((OWN, LEAF, HALF), F32),
            jax.ShapeDtypeStruct((OWN, LEAF, HALF), BF16),
        ),
        in_specs=[hbm_spec] * 12,
        out_specs=(vmem_spec, vmem_spec),
        scratch_shapes=[
            smem((2 * SLOTS, OWN), jnp.int32), smem((OWN,), jnp.int32),
            smem((4, OWN), jnp.int32), smem((MIDS, 4), jnp.int32),
            vmem((OWN + 1, LEAF, HALF), BF16),
            vmem((OWN + 1, LEAF, HALF), BF16),
            *[vmem((2, n, LEAF, HALF), BF16) for n in CHUNKS for _ in range(2)],
            vmem((OWN, SLOTS, LEAF, LEAF), BF16),
            vmem((OWN, RANK, LEAF), BF16),
            vmem((OWN, RANK, 4 * RANK), BF16),
            vmem((MIDS, RANK, 8 * RANK), BF16),
            vmem((MIDS, RANK, 4 * RANK), BF16),
            vmem((MIDS, RANK, RANK), BF16),
            vmem((OWN, LEAF, RANK), BF16),
            vmem((MIDS, 8 * RANK, RANK), BF16),
            vmem((MIDS, RANK, RANK), BF16),
            vmem((2, RANK, TOP_WIDTH), BF16),
            vmem((WINDOW, RANK, HALF), BF16),
            vmem((MID_WINDOW, RANK, HALF), BF16),
            vmem((RANK, HALF), BF16),
            vmem((COLUMNS, 2, RANK, HALF), BF16),
            vmem((RING, ROWS, HALF), BF16),
            vmem((RING, ROWS, HALF), BF16),
            vmem((GROUP, ROWS, HALF), BF16),
            vmem((OWN, RANK, HALF), F32),
            vmem((OWN, LEAF, HALF), BF16),
            dma((11,)), dma((4,)),
            dma(()), dma(()),
            dma((2, 4)), dma((2, 4)),
            dma((4,)), dma((4,)),
            dma((2,)), dma((2,)),
            dma((7,)), dma((7,)),
            dma((GROUP,)), dma((GROUP,)),
            dma((15,)), dma((15,)),
            dma((7,)), dma((7,)),
            dma((3,)), dma((3,)),
            dma((4, 2)), dma((4, 2)),
        ],
        compiler_params=pltpu.CompilerParams(
            collective_id=0, has_side_effects=True, vmem_limit_bytes=48 * 2**20
        ),
        name="h2_product",
    )(*[pltpu.with_memory_space_constraint(v, pltpu.MemorySpace.HBM) for v in operands])
    return (near + take.astype(F32)).reshape(OWN * LEAF, HALF)


def solution(mesh):
    return jax.shard_map(
        shards,
        mesh=mesh,
        in_specs=(
            P("leaf", "col"),
            P("leaf", "col", None, None),
            P("leaf", None),
            P("leaf"),
            P("leaf", None, None),
            P("leaf", None, None),
            P("leaf", None),
            P("leaf", None, None),
            P("leaf", None, None),
            P("leaf", None),
            P("leaf", None, None),
            P(),
        ),
        out_specs=P("leaf", "col"),
        check_vma=False,
    )
```

```python
import jax
import jax.numpy as jnp
from jax import lax
from jax.experimental import pallas as pl
from jax.experimental.pallas import tpu as pltpu
from jax.sharding import PartitionSpec as P

MESH = pl.DeviceIdType.MESH
F32 = jnp.float32
BF16 = jnp.bfloat16

LEAF = 256
RANK = 64
HALF = 128
OWN = 16
HALO = 8
MIDS = 2
GROUP = 4
RING = 8
COLUMNS = 16
SLOTS = 4
WINDOW = OWN + 2 * HALO
CHUNKS = (2, 2, 2, 2)
TOP_WIDTH = 2 * COLUMNS * RANK
ROWS = 2 * RANK // RING
MID_WINDOW = 4 * GROUP * MIDS


def dot(a, b):
    return jnp.dot(a, b, preferred_element_type=F32)


def by_fours(body):
    def step(k, _):
        for i in range(4):
            body(4 * k + i)
        return 0

    lax.fori_loop(0, OWN // 4, step, 0)


def kernel(
    src, tiles, near_index_in, near_count_in, basis, coupling, leaf_far_in, up_leaf, mid_coupling, mid_far_in, up_mid,
    top_coupling,
    near, take,
    near_index, near_count, leaf_far, mid_far,
    own0, own1, ha0, ha1, hb0, hb1, hc0, hc1, hd0, hd1, tile, bas, cpl, upl, mcp, upm, bat, upl_t, upm_t, top, coef, mid, part, top_b, field, top_c, rows, lfield, give,
    load_sem, tile_sem, sib_send, sib_recv, halo_send, halo_recv, fwd_send, fwd_recv, coef_send, coef_recv,
    mid_send, mid_recv, cross_send, cross_recv, b_send, b_recv, c_send, c_recv, d_send, d_recv, give_send, give_recv,
):
    d, c = lax.axis_index("leaf"), lax.axis_index("col")
    devices = COLUMNS * RING
    g, r = d // GROUP, d % GROUP
    column, z = d // RING, d % RING
    half, x, y = g % 2, column % 4, column // 4
    sibling = (d, 1 - c)
    after, before = ((d + 1) % devices, c), ((d + devices - 1) % devices, c)
    mates = [(g * GROUP + (r + o) % GROUP, c) for o in (1, 2, 3)]
    offsets = [(yo, xo) for yo in range(4) for xo in range(4) if yo or xo]
    peers = [((((y + yo) % 4) * 4 + (x + xo) % 4) * RING + z, c) for yo, xo in offsets]
    across = (((column + 1 - 2 * half + COLUMNS) % COLUMNS) * RING + z, c)
    across_from = (((column - 1 + 2 * half + COLUMNS) % COLUMNS) * RING + z, c)

    def copy(a, b, send, recv, device):
        return pltpu.make_async_remote_copy(
            src_ref=a, dst_ref=b, send_sem=send, recv_sem=recv, device_id=device, device_id_type=MESH
        )

    barrier = pltpu.get_barrier_semaphore()

    def greet(device):
        pl.semaphore_signal(barrier, inc=1, device_id=device, device_id_type=MESH)

    column_mates = [(column * RING + (z + o) % RING, c) for o in range(1, RING)]
    greeted = [sibling, after, before, across, across_from] + column_mates + peers
    for device in greeted:
        greet(device)

    loads = [
        pltpu.make_async_copy(src, own0.at[pl.ds(0, OWN)], load_sem.at[0]),
        pltpu.make_async_copy(basis, bas, load_sem.at[1]),
        pltpu.make_async_copy(up_leaf, upl, load_sem.at[2]),
        pltpu.make_async_copy(up_mid, upm, load_sem.at[3]),
        pltpu.make_async_copy(leaf_far_in, leaf_far, load_sem.at[4]),
        pltpu.make_async_copy(mid_far_in, mid_far, load_sem.at[5]),
        pltpu.make_async_copy(near_index_in, near_index, load_sem.at[6]),
        pltpu.make_async_copy(near_count_in, near_count, load_sem.at[7]),
        pltpu.make_async_copy(coupling, cpl, load_sem.at[8]),
        pltpu.make_async_copy(mid_coupling, mcp, load_sem.at[9]),
    ]
    loads.append(pltpu.make_async_copy(top_coupling.at[pl.ds(2 * column, 2)], top, load_sem.at[10]))
    for load in loads:
        load.start()
    tile_loads = [
        pltpu.make_async_copy(tiles.at[pl.ds(4 * k, 4)], tile.at[pl.ds(4 * k, 4)], tile_sem.at[k]) for k in range(4)
    ]
    for load in tile_loads:
        load.start()

    zero = jnp.zeros((LEAF, HALF), BF16)
    own0[OWN] = zero
    own1[OWN] = zero
    for n in range(COLUMNS):
        top_b[n, 1 - half] = jnp.zeros((RANK, HALF), BF16)
    pl.semaphore_wait(barrier, len(greeted))

    to_sibling = copy(src, own1.at[pl.ds(0, OWN)], sib_send, sib_recv, sibling)
    halos, forwards = [], []
    done = 0
    for i, (h0, h1) in enumerate(((ha0, ha1), (hb0, hb1), (hc0, hc1), (hd0, hd1))):
        n = CHUNKS[i]
        halos.append(
            (
                copy(src.at[pl.ds(OWN - done - n, n)], h0.at[0], halo_send.at[0, i], halo_recv.at[0, i], after),
                copy(src.at[pl.ds(done, n)], h0.at[1], halo_send.at[1, i], halo_recv.at[1, i], before),
            )
        )
        forwards.append(copy(h0, h1, fwd_send.at[i], fwd_recv.at[i], sibling))
        done += n

    def forward(i):
        for one in halos[i]:
            one.wait_recv()
        forwards[i].start()

    for one in halos[0]:
        one.start()
    to_sibling.start()

    loads[0].wait()
    loads[1].wait()

    def leaf_step(i):
        coef[HALO + i] = dot(bas[i], own0[i]).astype(BF16)

    by_fours(leaf_step)
    coef_out = [
        copy(coef.at[pl.ds(OWN, HALO)], coef.at[pl.ds(0, HALO)], coef_send.at[0], coef_recv.at[0], after),
        copy(coef.at[pl.ds(HALO, HALO)], coef.at[pl.ds(HALO + OWN, HALO)], coef_send.at[1], coef_recv.at[1], before),
    ]

    loads[2].wait()
    loads[3].wait()
    base = GROUP * MIDS
    values = [
        dot(upl[q], coef[pl.ds(HALO + 8 * q, 8)].reshape(8 * RANK, HALF)).astype(BF16) for q in range(MIDS)
    ]
    lifts = [dot(upm[q], values[q]).astype(BF16).astype(F32) for q in range(MIDS)]
    part[...] = (lifts[0] + lifts[1]).astype(BF16)
    for q in range(MIDS):
        mid[base + MIDS * z + q] = values[q]

    to_peers = []
    for n, (yo, xo) in enumerate(offsets):
        back = offsets.index(((4 - yo) % 4, (4 - xo) % 4))
        to_peers.append(copy(part, top_b.at[column, half], b_send.at[n], b_recv.at[back], peers[n]))

    def near_z(o):
        return (column * RING + (z + o + RING) % RING, c)

    def of(o):
        return mid.at[pl.ds(base + MIDS * ((z + o + RING) % RING), MIDS)]

    up = 1 - 2 * c
    steps = [(0, 1), (0, -1), (0, 2), (0, -2), (-2, 1), (2, -1), (-2 * up, 2 * up)]
    mid_out = [
        copy(of(whose), of(whose), mid_send.at[n], mid_recv.at[n], near_z(o)) for n, (whose, o) in enumerate(steps)
    ]
    mid_got = [
        copy(of(whose - o), of(whose - o), mid_send.at[n], mid_recv.at[n], near_z(o))
        for n, (whose, o) in enumerate(steps)
    ]

    def cross(o):
        member = (z + o + RING) % GROUP
        there = mid.at[pl.ds(3 * base * half + MIDS * member, MIDS)]
        return copy(of(o), there, cross_send.at[member], cross_recv.at[member], across)

    def send_across(offsets):
        for o in offsets:
            pl.when(((z + o + RING) % RING) // GROUP != half)(cross(o).start)

    for n in range(4):
        mid_out[n].start()
    for one in to_peers:
        one.start()
    for one in coef_out:
        one.start()
    top_b[column, half] = part[...]

    for one in halos[1]:
        one.start()
    for n in (2, 3):
        mid_got[n].wait_recv()
    for n in (4, 5, 6):
        mid_out[n].start()
    for n in (0, 1):
        mid_got[n].wait_recv()
    send_across((1, -1, 2, -2))

    def turn(i):
        bat[i] = bas[i].T

    by_fours(turn)
    for q in range(MIDS):
        upl_t[q] = upl[q].T
        upm_t[q] = upm[q].T
    loads[4].wait()
    loads[8].wait()
    for one in coef_out:
        one.wait_recv()

    def far_step(i):
        picked = [coef[jnp.clip(leaf_far[f, i] - (d * OWN - HALO), 0, WINDOW - 1)] for f in range(4)]
        lfield[i] = dot(cpl[i], jnp.concatenate(picked, axis=0))

    by_fours(far_step)

    loads[10].wait()
    lanes = pl.ds(pl.multiple_of(column * 2 * RANK, 2 * RANK), 2 * RANK)
    itself = lax.broadcasted_iota(jnp.int32, (RANK, 2 * RANK), 1) // RANK == half
    top[half, :, lanes] = jnp.where(itself, 0.0, top[half, :, lanes].astype(F32)).astype(BF16)

    for n in range(len(peers)):
        yo, xo = offsets[n]
        from_column = ((y + yo) % 4) * 4 + (x + xo) % 4
        copy(part, top_b.at[from_column, half], b_send.at[n], b_recv.at[n], sibling).wait_recv()
    total = dot(top[...].reshape(2 * RANK, TOP_WIDTH), top_b[...].reshape(TOP_WIDTH, HALF))
    field[...] = total.astype(BF16).reshape(RING, ROWS, HALF)
    fields_out = []
    for o in range(1, RING):
        there = (z + o) % RING
        fields_out.append(
            copy(field.at[there], top_c.at[o], c_send.at[o - 1], c_recv.at[o - 1], column_mates[o - 1])
        )
    for one in fields_out:
        one.start()
    for one in halos[2]:
        one.start()
    for one in halos[3]:
        one.start()
    for n in (4, 5, 6):
        mid_got[n].wait_recv()
    send_across((3, -3, 4))
    for one in fields_out:
        one.wait_recv()
    reduced = field[z].astype(F32)
    for o in range(1, RING):
        reduced = reduced + top_c[o].astype(F32)
    rows[r] = reduced.astype(BF16)
    rows_out = [copy(rows.at[r], rows.at[r], d_send.at[o], d_recv.at[o], mates[o]) for o in range(3)]
    for one in rows_out:
        one.start()

    reach = [(ha0, ha1, 6, 18), (hb0, hb1, 4, 22), (hc0, hc1, 2, 26), (hd0, hd1, 0, 30)]
    batches = [(6, 2, 2), (4, 6, 2), (2, 10, 2), (0, 14, 2)]

    def give_copy(phase, k):
        first, step, n = batches[phase]
        here = pl.ds(first + step * k, n)
        return copy(give.at[here], take.at[here], give_send.at[phase, k], give_recv.at[phase, k], sibling)

    def near_rows(i, s, k, phase):
        slot = c * SLOTS + s
        j = near_index[slot, i] - (d * OWN - HALO)
        live = slot < near_count[i]
        inside = jnp.logical_and(live, jnp.logical_and(j >= HALO, j < HALO + OWN))
        m = jnp.where(inside, jnp.clip(j - HALO, 0, OWN - 1), OWN)
        low, high = own0[m], own1[m]
        for p in range(phase + 1):
            h0, h1, first, step = reach[p]
            m = j - (first + step * k)
            inside = jnp.logical_and(live, jnp.logical_and(m >= 0, m < CHUNKS[p]))
            m = jnp.clip(m, 0, CHUNKS[p] - 1)
            low, high = jnp.where(inside, h0[k, m], low), jnp.where(inside, h1[k, m], high)
        return jnp.concatenate([low, high], axis=1)

    def near_phase(phase, fresh=False):
        forwards[phase].wait_recv()
        first, step, n = batches[phase]

        def side(k, _):
            for i in range(n):
                leaf = first + step * k + i
                terms = [dot(tile[leaf, s], near_rows(leaf, s, k, phase)) for s in range(SLOTS)]
                total = (terms[0] + terms[1]) + (terms[2] + terms[3])
                give[leaf] = total[:, HALF:].astype(BF16)
                near[leaf] = total[:, :HALF] if fresh else near[leaf] + total[:, :HALF]
            give_copy(phase, k).start()
            return 0

        lax.fori_loop(0, 2, side, 0)

    loads[6].wait()
    loads[7].wait()
    to_sibling.wait_recv()
    for load in tile_loads:
        load.wait()

    forward(0)
    forward(1)
    near_phase(0, True)
    near_phase(1, True)
    for n in range(3):
        got = rows.at[(r + 3 - n) % GROUP]
        copy(got, got, d_send.at[n], d_recv.at[n], sibling).wait_recv()
    top_field = rows[...].reshape(RANK, HALF)
    lifted = [dot(upm_t[q], top_field) for q in range(MIDS)]

    loads[5].wait()
    loads[9].wait()
    for n in range(GROUP):
        got = mid.at[pl.ds(3 * base * half + MIDS * n, MIDS)]
        copy(got, got, cross_send.at[n], cross_recv.at[n], across).wait_recv()
    first = column * RING * MIDS - base
    for q in range(MIDS):
        picked = [mid[jnp.clip(mid_far[q, f] - first, 0, MID_WINDOW - 1)] for f in range(4)]
        value = (dot(mcp[q], jnp.concatenate(picked, axis=0)) + lifted[q]).astype(BF16)
        down = dot(upl_t[q], value).reshape(8, RANK, HALF)
        lfield[pl.ds(8 * q, 8)] = lfield[pl.ds(8 * q, 8)] + down

    forward(2)

    def product_step(k, _):
        for i in range(4):
            inner_leaf, outer_leaf = 4 + 4 * k + i, 12 * k + i
            near[inner_leaf] = near[inner_leaf] + dot(bat[inner_leaf], lfield[inner_leaf].astype(BF16))
            near[outer_leaf] = dot(bat[outer_leaf], lfield[outer_leaf].astype(BF16))
        return 0

    lax.fori_loop(0, 2, product_step, 0)

    forward(3)
    near_phase(2)
    near_phase(3)

    for phase in range(4):
        for k in range(2):
            give_copy(phase, k).wait()
    to_sibling.wait_send()
    for one in [one for pair in halos for one in pair] + forwards + coef_out + mid_out + to_peers + fields_out + rows_out:
        one.wait_send()
    for n in range(GROUP):
        cross(4 - r + n).wait_send()


def shards(
    sources, near_tiles, near_index, near_count, leaf_basis, leaf_coupling, leaf_far, up_leaf, mid_coupling, mid_far,
    up_mid, top_coupling,
):
    hbm_spec = pl.BlockSpec(memory_space=pltpu.MemorySpace.HBM)
    vmem_spec = pl.BlockSpec(memory_space=pltpu.MemorySpace.VMEM)
    dma, vmem, smem = pltpu.SemaphoreType.DMA, pltpu.VMEM, pltpu.SMEM
    operands = [
        sources.reshape(OWN, LEAF, HALF), near_tiles, near_index.T, near_count, leaf_basis, leaf_coupling, leaf_far.T,
        up_leaf, mid_coupling, mid_far, up_mid, top_coupling,
    ]
    near, take = pl.pallas_call(
        kernel,
        out_shape=(
            jax.ShapeDtypeStruct((OWN, LEAF, HALF), F32),
            jax.ShapeDtypeStruct((OWN, LEAF, HALF), BF16),
        ),
        in_specs=[hbm_spec] * 12,
        out_specs=(vmem_spec, vmem_spec),
        scratch_shapes=[
            smem((2 * SLOTS, OWN), jnp.int32), smem((OWN,), jnp.int32),
            smem((4, OWN), jnp.int32), smem((MIDS, 4), jnp.int32),
            vmem((OWN + 1, LEAF, HALF), BF16),
            vmem((OWN + 1, LEAF, HALF), BF16),
            *[vmem((2, n, LEAF, HALF), BF16) for n in CHUNKS for _ in range(2)],
            vmem((OWN, SLOTS, LEAF, LEAF), BF16),
            vmem((OWN, RANK, LEAF), BF16),
            vmem((OWN, RANK, 4 * RANK), BF16),
            vmem((MIDS, RANK, 8 * RANK), BF16),
            vmem((MIDS, RANK, 4 * RANK), BF16),
            vmem((MIDS, RANK, RANK), BF16),
            vmem((OWN, LEAF, RANK), BF16),
            vmem((MIDS, 8 * RANK, RANK), BF16),
            vmem((MIDS, RANK, RANK), BF16),
            vmem((2, RANK, TOP_WIDTH), BF16),
            vmem((WINDOW, RANK, HALF), BF16),
            vmem((MID_WINDOW, RANK, HALF), BF16),
            vmem((RANK, HALF), BF16),
            vmem((COLUMNS, 2, RANK, HALF), BF16),
            vmem((RING, ROWS, HALF), BF16),
            vmem((RING, ROWS, HALF), BF16),
            vmem((GROUP, ROWS, HALF), BF16),
            vmem((OWN, RANK, HALF), F32),
            vmem((OWN, LEAF, HALF), BF16),
            dma((11,)), dma((4,)),
            dma(()), dma(()),
            dma((2, 4)), dma((2, 4)),
            dma((4,)), dma((4,)),
            dma((2,)), dma((2,)),
            dma((7,)), dma((7,)),
            dma((GROUP,)), dma((GROUP,)),
            dma((15,)), dma((15,)),
            dma((7,)), dma((7,)),
            dma((3,)), dma((3,)),
            dma((4, 2)), dma((4, 2)),
        ],
        compiler_params=pltpu.CompilerParams(
            collective_id=0, has_side_effects=True, vmem_limit_bytes=48 * 2**20
        ),
        name="h2_product",
    )(*[pltpu.with_memory_space_constraint(v, pltpu.MemorySpace.HBM) for v in operands])
    return (near + take.astype(F32)).reshape(OWN * LEAF, HALF)


def solution(mesh):
    return jax.shard_map(
        shards,
        mesh=mesh,
        in_specs=(
            P("leaf", "col"),
            P("leaf", "col", None, None),
            P("leaf", None),
            P("leaf"),
            P("leaf", None, None),
            P("leaf", None, None),
            P("leaf", None),
            P("leaf", None, None),
            P("leaf", None, None),
            P("leaf", None),
            P("leaf", None, None),
            P(),
        ),
        out_specs=P("leaf", "col"),
        check_vma=False,
    )
```
